32 devices in a mesh: section: 8 (over y, x, core), dp: 4 (over z).
Axes of the slice: x: 2, y: 2, z: 4, core: 2. Of those that a mesh axis runs over, the one named last changes fastest.
Arguments:
- inputs: bfloat16 [4, 8, 128, 4096], P('dp', 'section'), may hold values from -6 to 6
- key_rows: bfloat16 [4, 8, 24, 4096], P('dp', None, None, 'section'), may hold values from -32 to 32
- value_rows: bfloat16 [4, 8, 24, 4096], P('dp', None, None, 'section'), may hold values from -6 to 6
- query_gain: float32 [8, 4096], P('section'), may hold values from 0.1 to 1.9
- cotangent: bfloat16 [4, 8, 128, 4096], P('dp', 'section'), may hold values from -6 to 6
Outputs:
- key_grads: bfloat16 [4, 8, 24, 4096], P('dp', None, None, 'section')
- value_grads: bfloat16 [4, 8, 24, 4096], P('dp', None, None, 'section')
- gain_grads: float32 [8, 4096], P('section')
The draws below stay inside these ranges and needn't reach their ends.
All inputs are finite; a program needn't handle non-finite values.
Results may differ from the reference program's by a relative error of at most 0.008.
Values may be sent and summed in bfloat16 or wider, within the bound.
A program may use at most 64 MiB of HBM per device.

```python
import jax
import jax.numpy as jnp
from jax import lax

D = 4096
HEAD = 64
TOK = 128
SRC = 24
TICKS = 3
LAYERS = 8
DOCS = 4


def draw_inputs(key, part):
    noise_key = jax.random.fold_in(key, 7002)
    drawn = jnp.clip(jax.random.normal(noise_key, (DOCS, LAYERS, TOK, D), jnp.float32), -6.0, 6.0)
    return drawn.astype(jnp.bfloat16)


def draw_key_rows(key, part):
    base = jnp.clip(jax.random.normal(jax.random.fold_in(key, 7011), (DOCS, LAYERS, SRC, D), jnp.float32), -6.0, 6.0)
    return base.astype(jnp.bfloat16)


def block_scale(key, shape, cuts, least, largest):
    loudness = 1.0
    for position, shards_of in cuts:
        steps = jax.random.uniform(jax.random.fold_in(jax.random.fold_in(key, 6), position), (shards_of,), jnp.float32, least / len(cuts), largest / len(cuts))
        loudness = loudness * jnp.repeat(jnp.exp(steps), shape[position] // shards_of).reshape((-1,) + (1,) * (len(shape) - 1 - position))
    return loudness


def scatter_about(key, extent, scale, most, shards=(), dtype=jnp.bfloat16):
    values = jax.random.normal(key, extent, jnp.float32) * scale
    if len(shards) > 0:
        values = block_scale(key, extent, shards, -0.22, 0.18) * values
    return jnp.clip(values, min=-most, max=most).astype(dtype)


def setup_inputs(seed: int = 0) -> dict:
    arg_keys = jax.random.split(jax.random.key(seed), 6)
    inputs = draw_inputs(jax.random.fold_in(arg_keys[5], 71), 0)
    key_rows = draw_key_rows(jax.random.fold_in(arg_keys[5], 71), 0)
    value_rows = scatter_about(arg_keys[2], (DOCS, LAYERS, SRC, D), 1.0, 6.0, ((0, 4), (3, 8)))
    query_gain = jnp.clip(1.0 + 0.18 * jax.random.normal(arg_keys[3], (LAYERS, D), jnp.float32), 0.1, 1.9)
    cotangent = scatter_about(arg_keys[4], (DOCS, LAYERS, TOK, D), 1.0, 6.0, ((0, 4), (1, 8)))
    return {"inputs": inputs, "key_rows": key_rows, "value_rows": value_rows, "query_gain": query_gain, "cotangent": cotangent}


def product(form, left, right):
    return jnp.einsum(form, left.astype(jnp.float32), right.astype(jnp.float32))

def attend_forward(states, gain_row, key_block, value_block):
    floats = states.astype(jnp.float32)
    inverse = lax.rsqrt(lax.optimization_barrier(jnp.mean(floats * floats, axis=-1, keepdims=True)) + 1e-06)
    queries = (floats * inverse * gain_row).astype(jnp.bfloat16)
    tok_rows, width = states.shape
    src_rows = key_block.shape[0]
    heads_count = width // HEAD
    query_heads = queries.reshape(tok_rows, heads_count, HEAD)
    key_heads = key_block.reshape(src_rows, heads_count, HEAD)
    value_heads = value_block.reshape(src_rows, heads_count, HEAD)
    scores = product('shd,thd->hst', key_heads, query_heads) * HEAD ** (-0.5)
    highest = lax.optimization_barrier(jnp.max(scores, axis=1, keepdims=True))
    weights = jnp.exp(scores - highest)
    probs = weights / lax.optimization_barrier(jnp.sum(weights, axis=1, keepdims=True))
    probs_low = probs.astype(jnp.bfloat16)
    mixed = product('hst,shd->thd', probs_low, value_heads).reshape(tok_rows, width)
    produced = (floats + mixed).astype(jnp.bfloat16)
    return (produced, (inverse, queries, probs, probs_low))

def attend_backward(states, gain_row, key_block, value_block, saved, incoming, needed):
    inverse, queries, probs, probs_low = saved
    tok_rows, width = states.shape
    src_rows = key_block.shape[0]
    heads_count = width // HEAD
    query_heads = queries.reshape(tok_rows, heads_count, HEAD)
    key_heads = key_block.reshape(src_rows, heads_count, HEAD)
    value_heads = value_block.reshape(src_rows, heads_count, HEAD)
    grad_heads = incoming.reshape(tok_rows, heads_count, HEAD)
    dprob = product('shd,thd->hst', value_heads, grad_heads)
    dscore = (probs * (dprob - lax.optimization_barrier(jnp.sum(probs * dprob, axis=1, keepdims=True))) * HEAD ** (-0.5)).astype(jnp.bfloat16)
    value_step = product('hst,thd->shd', probs_low, grad_heads).reshape(src_rows, width)
    key_step = product('hst,thd->shd', dscore, query_heads).reshape(src_rows, width)
    dquery = product('hst,shd->thd', dscore, key_heads).reshape(tok_rows, width)
    unit = states.astype(jnp.float32) * inverse
    gain_step = lax.optimization_barrier(jnp.sum(dquery * unit, axis=0))
    if needed:
        scaled = gain_row * dquery
        back = incoming.astype(jnp.float32) + inverse * (scaled - unit * lax.optimization_barrier(jnp.mean(scaled * unit, axis=-1, keepdims=True)))
        back = back.astype(jnp.bfloat16)
    else:
        back = None
    return (back, key_step, value_step, gain_step)

def per_document(inputs_doc, keys_doc, values_doc, cot_doc, query_gain):
    forward = jax.vmap(attend_forward)
    current = inputs_doc
    states = [current]
    for tick_index in range(TICKS - 1):
        produced, unused = forward(current, query_gain, keys_doc, values_doc)
        current = jnp.roll(produced, 1, axis=0)
        states.append(current)
    key_total = jnp.zeros(keys_doc.shape, jnp.float32)
    value_total = jnp.zeros(values_doc.shape, jnp.float32)
    gain_total = jnp.zeros(query_gain.shape, jnp.float32)
    carried = cot_doc
    for tick_index in range(TICKS - 1, -1, -1):
        incoming = jnp.roll(carried, -1, axis=0)
        unused, saved = forward(states[tick_index], query_gain, keys_doc, values_doc)
        needed = tick_index > 0
        backward = jax.vmap(lambda a, b, c, e, f, g: attend_backward(a, b, c, e, f, g, needed))
        carried, key_step, value_step, gain_step = backward(states[tick_index], query_gain, keys_doc, values_doc, saved, incoming)
        key_total = key_total + key_step
        value_total = value_total + value_step
        gain_total = gain_total + gain_step
    return (key_total.astype(jnp.bfloat16), value_total.astype(jnp.bfloat16), gain_total)

def reference(inputs, key_rows, value_rows, query_gain, cotangent):

    def one_doc(packed):
        return per_document(packed[0], packed[1], packed[2], packed[3], query_gain)
    key_grads, value_grads, gain_parts = lax.map(one_doc, (inputs, key_rows, value_rows, cotangent))
    return (key_grads, value_grads, lax.optimization_barrier(jnp.sum(gain_parts, axis=0)))
```

```python
import functools

import jax
import jax.numpy as jnp
from jax import lax
from jax.experimental import pallas as pl
from jax.experimental.pallas import tpu as pltpu
from jax.sharding import PartitionSpec as P

HEAD = 64
TICKS = 3
LANES = 128
MESH = pl.DeviceIdType.MESH
F32 = jnp.float32
BF16 = jnp.bfloat16


def nn(a, b):
    return lax.dot_general(a, b, (((1,), (0,)), ((), ())), preferred_element_type=F32)


def nt(a, b):
    return lax.dot_general(a, b, (((1,), (1,)), ((), ())), preferred_element_type=F32)


def kernel(
    n, ndp, unroll,
    x_ref, ct_ref, k_ref, v_ref, g_ref,
    kout_ref, vout_ref, gout_ref,
    xin, cin, gin, stat, kd, vd, kdt, vdt, gt, xs, qs, probs, plow, raws, ds, grads,
    red, inv, ar, ktot, vtot, gsend, gmid, gdp,
    x_send, x_recv, c_send, c_recv, g_send, g_recv, st_send, st_recv,
    ar_send, ar_recv, gm_send, gm_recv, dp_send, dp_recv, loc,
):
    me = lax.axis_index("section")
    doc = lax.axis_index("dp")
    tok, width = x_ref.shape
    src, cols = k_ref.shape[1], k_ref.shape[2]
    blocks = cols // LANES
    per = LANES // HEAD
    brow = per * src
    scale = HEAD ** (-0.5)

    def peers(body):
        def step(j, c):
            body(lax.rem(me + j, n))
            return c
        lax.fori_loop(1, n, step, 0)

    def docs(body):
        def step(j, c):
            body(lax.rem(doc + j, ndp))
            return c
        lax.fori_loop(1, ndp, step, 0)

    def each(body, u=None):
        def step(m, c):
            body(m)
            return c
        lax.fori_loop(0, n, step, 0, unroll=u or unroll)

    def to(p, source, target, send, recv):
        return pltpu.make_async_remote_copy(
            src_ref=source, dst_ref=target, send_sem=send, recv_sem=recv,
            device_id={"section": p}, device_id_type=MESH)

    def to_doc(p, source, target, send, recv):
        return pltpu.make_async_remote_copy(
            src_ref=source, dst_ref=target, send_sem=send, recv_sem=recv,
            device_id={"dp": p}, device_id_type=MESH)

    def cut(ref, p):
        return ref.at[:, pl.ds(pl.multiple_of(p * cols, LANES), cols)]

    def x_copy(p, slot):
        return to(p, cut(x_ref, p), xin.at[slot], x_send.at[p], x_recv.at[slot])

    def c_copy(p, slot):
        return to(p, cut(ct_ref, p), cin.at[slot], c_send.at[p], c_recv.at[slot])

    def g_copy(p, slot):
        return to(p, cut(g_ref, p), gin.at[slot], g_send.at[p], g_recv.at[slot])

    def st_copy(p, slot):
        return to(p, stat.at[me], stat.at[slot], st_send.at[p], st_recv.at[slot])

    def ar_copy(a, p, slot):
        return to(p, ar.at[a, me], ar.at[a, slot], ar_send.at[a, p], ar_recv.at[a, slot])

    def gm_copy(p, slot):
        return to(p, gsend.at[p], gmid.at[slot], gm_send.at[p], gm_recv.at[slot])

    def dp_copy(p, slot):
        return to_doc(p, gmid, gdp.at[slot], dp_send.at[p], dp_recv.at[slot])

    barrier = pltpu.get_barrier_semaphore()
    peers(lambda p: pl.semaphore_signal(barrier, inc=1, device_id={"section": p}, device_id_type=MESH))
    docs(lambda p: pl.semaphore_signal(barrier, inc=1, device_id={"dp": p}, device_id_type=MESH))
    pl.semaphore_wait(barrier, n + ndp - 2)

    peers(lambda p: g_copy(p, me).start())
    peers(lambda p: x_copy(p, me).start())
    own = [
        pltpu.make_async_copy(cut(g_ref, me), gin.at[me], loc.at[0]),
        pltpu.make_async_copy(cut(x_ref, me), xin.at[me], loc.at[1]),
        pltpu.make_async_copy(cut(ct_ref, me), cin.at[me], loc.at[2]),
    ]
    for copy in own:
        copy.start()

    total = jnp.zeros((tok, LANES), F32)
    for b in range(width // LANES):
        part = x_ref[:, b * LANES:(b + 1) * LANES].astype(F32)
        total = total + part * part
    stat[me] = jnp.sum(total.T, axis=0, keepdims=True)
    peers(lambda p: st_copy(p, me).start())
    peers(lambda p: c_copy(p, me).start())

    lane = lax.broadcasted_iota(jnp.int32, (src, LANES), 1)
    sides = [jnp.logical_and(lane >= i * HEAD, lane < (i + 1) * HEAD) for i in range(per)]

    def spread(l):
        for source, plain, turned in ((k_ref, kd, kdt), (v_ref, vd, vdt)):
            rows = source[l].astype(F32)
            for b in range(blocks):
                piece = rows[:, b * LANES:(b + 1) * LANES]
                both = jnp.concatenate([jnp.where(s, piece, 0.0) for s in sides], axis=0)
                plain[l, b] = both.astype(BF16)
                turned[l, b] = both.T.astype(BF16)
        ktot[l] = jnp.zeros((src, cols), F32)
        vtot[l] = jnp.zeros((src, cols), F32)

    each(spread, 1)

    own[0].wait()
    peers(lambda p: g_copy(p, p).wait_recv())

    def turn_gain(l):
        for b in range(blocks):
            row = gin[l, :, b * LANES:(b + 1) * LANES]
            gt[l, b * LANES:(b + 1) * LANES, :] = jnp.broadcast_to(row, (LANES, LANES)).T

    each(turn_gain, 1)
    stats_done = peers(lambda p: st_copy(p, p).wait_recv())

    def fwd(k, m, more):
        l = lax.rem(m + k, n)
        factor = inv[k, m]
        pieces = []
        sums = jnp.zeros((1, tok), F32)
        for b in range(blocks):
            at = slice(b * LANES, (b + 1) * LANES)
            rows = slice(b * brow, (b + 1) * brow)
            xf = xs[k, m, at, :].astype(F32)
            q = (xf * factor * gt[l, at, :]).astype(BF16)
            qs[k, m, at, :] = q
            raw = nn(kd[l, b], q)
            raws[k, m, rows, :] = raw
            s3 = raw.reshape(per, src, tok) * scale
            w = jnp.exp(s3 - jnp.max(s3, axis=1, keepdims=True))
            p = w * (1.0 / jnp.sum(w, axis=1, keepdims=True))
            p = p.reshape(brow, tok)
            probs[k, m, rows, :] = p
            low = p.astype(BF16)
            plow[k, m, rows, :] = low
            if more:
                y = (xf + nn(vdt[l, b], low)).astype(BF16)
                xs[k + 1, m, at, :] = y
                yf = y.astype(F32)
                sums = sums + jnp.sum(yf * yf, axis=0, keepdims=True)
        if more:
            ar[k, me, m] = sums

    def reduced(a):
        peers(lambda p: ar_copy(a, p, p).wait_recv())
        total = ar[a, 0]
        for s in range(1, n):
            total = total + ar[a, s]
        return total * (1.0 / width)

    def arrive(j, c):
        m = lax.rem(me + j, n)

        @pl.when(j == 0)
        def _():
            own[1].wait()

        @pl.when(j > 0)
        def _():
            x_copy(m, m).wait_recv()

        inv[0, m] = lax.rsqrt(stat[m] * (1.0 / width) + 1e-6)
        for b in range(blocks):
            at = slice(b * LANES, (b + 1) * LANES)
            xs[0, m, at, :] = xin[m, :, at].T
        fwd(0, m, True)
        return c

    lax.fori_loop(0, n, arrive, 0)
    for k in range(1, TICKS):
        peers(lambda p: ar_copy(k - 1, p, me).start())
        inv[k] = lax.rsqrt(reduced(k - 1) + 1e-6)
        each(lambda m: fwd(k, m, k + 1 < TICKS))

    def arrive_c(j, c):
        s = lax.rem(me + j, n)

        @pl.when(j == 0)
        def _():
            own[2].wait()

        @pl.when(j > 0)
        def _():
            c_copy(s, s).wait_recv()

        m = lax.rem(s + TICKS * n - TICKS, n)
        for b in range(blocks):
            at = slice(b * LANES, (b + 1) * LANES)
            grads[m, at, :] = cin[s, :, at].T
        return c

    lax.fori_loop(0, n, arrive_c, 0)

    def scores_back(k, a, m):
        l = lax.rem(m + k, n)
        sums = jnp.zeros((1, tok), F32)
        for b in range(blocks):
            at = slice(b * LANES, (b + 1) * LANES)
            rows = slice(b * brow, (b + 1) * brow)
            dprob = nn(vd[l, b], grads[m, at, :]).reshape(per, src, tok)
            p = probs[k, m, rows, :].reshape(per, src, tok)
            mean = jnp.sum(p * dprob, axis=1, keepdims=True)
            d = (p * (dprob - mean) * scale).reshape(brow, tok).astype(BF16)
            ds[m, rows, :] = d
            if a is not None:
                sums = sums + jnp.sum(d.astype(F32) * raws[k, m, rows, :], axis=0, keepdims=True)
        if a is not None:
            ar[a, me, m] = sums

    def picked(r):
        out = r[:src]
        for i in range(1, per):
            out = jnp.where(sides[i], r[i * src:(i + 1) * src], out)
        return out

    def key_step(k, m):
        l = lax.rem(m + k, n)
        for b in range(blocks):
            at = slice(b * LANES, (b + 1) * LANES)
            rows = slice(b * brow, (b + 1) * brow)
            ktot[l, :, at] += picked(nt(ds[m, rows, :], qs[k, m, at, :]))

    def value_step(k, m):
        l = lax.rem(m + k, n)
        for b in range(blocks):
            at = slice(b * LANES, (b + 1) * LANES)
            rows = slice(b * brow, (b + 1) * brow)
            vtot[l, :, at] += picked(nt(plow[k, m, rows, :], grads[m, at, :]))

    def input_back(k, m):
        l = lax.rem(m + k, n)
        factor = inv[k, m]
        mean = red[m]
        for b in range(blocks):
            at = slice(b * LANES, (b + 1) * LANES)
            rows = slice(b * brow, (b + 1) * brow)
            dq = nn(kdt[l, b], ds[m, rows, :])
            u = xs[k, m, at, :].astype(F32) * factor
            back = grads[m, at, :].astype(F32) + factor * (gt[l, at, :] * dq - u * mean)
            grads[m, at, :] = back.astype(BF16)

    for k in range(TICKS - 1, 0, -1):
        a = TICKS - 1 + k - 1
        each(lambda m: scores_back(k, a, m))
        peers(lambda p: ar_copy(a, p, me).start())

        def filler(m):
            key_step(k, m)
            value_step(k, m)

        each(filler)
        red[...] = reduced(a)
        each(lambda m: input_back(k, m))

    def last(m):
        scores_back(0, None, m)
        key_step(0, m)
        steps = ktot[m]
        kout_ref[m] = steps.astype(BF16)
        gsend[m] = jnp.sum(steps * k_ref[m].astype(F32), axis=0, keepdims=True) / gin[m]

    each(last)
    peers(lambda p: gm_copy(p, me).start())
    gmid[me] = gsend[me]

    def finish(m):
        value_step(0, m)
        vout_ref[m] = vtot[m].astype(BF16)

    each(finish)
    peers(lambda p: gm_copy(p, p).wait_recv())
    docs(lambda p: dp_copy(p, doc).start())

    def drain(p):
        x_copy(p, me).wait_send()
        c_copy(p, me).wait_send()
        g_copy(p, me).wait_send()
        st_copy(p, me).wait_send()
        for a in range(2 * (TICKS - 1)):
            ar_copy(a, p, me).wait_send()
        gm_copy(p, me).wait_send()

    peers(drain)
    gdp[doc] = gmid[...]
    docs(lambda p: dp_copy(p, p).wait_recv())
    docs(lambda p: dp_copy(p, doc).wait_send())
    for s in range(n):
        out = gdp[0, s]
        for d in range(1, ndp):
            out = out + gdp[d, s]
        gout_ref[:, s * cols:(s + 1) * cols] = out


def on_device(inputs, key_rows, value_rows, query_gain, cotangent):
    n = lax.axis_size("section")
    ndp = lax.axis_size("dp")
    tok, width = inputs.shape[2:]
    src, cols = key_rows.shape[2:]
    blocks = cols // LANES
    brow = LANES // HEAD * src
    rows = blocks * brow
    rounds = 2 * (TICKS - 1)
    vmem = pltpu.VMEM
    sem = pltpu.SemaphoreType.DMA
    scratch = [
        vmem((n, tok, cols), BF16), vmem((n, tok, cols), BF16),
        vmem((n, 1, cols), F32), vmem((n, 1, tok), F32),
        vmem((n, blocks, brow, LANES), BF16), vmem((n, blocks, brow, LANES), BF16),
        vmem((n, blocks, LANES, brow), BF16), vmem((n, blocks, LANES, brow), BF16),
        vmem((n, cols, LANES), F32),
        vmem((TICKS, n, cols, tok), BF16), vmem((TICKS, n, cols, tok), BF16),
        vmem((TICKS, n, rows, tok), F32), vmem((TICKS, n, rows, tok), BF16),
        vmem((TICKS, n, rows, tok), F32),
        vmem((n, rows, tok), BF16), vmem((n, cols, tok), BF16),
        vmem((n, 1, tok), F32), vmem((TICKS, n, 1, tok), F32),
        vmem((rounds, n, n, 1, tok), F32),
        vmem((n, src, cols), F32), vmem((n, src, cols), F32),
        vmem((n, 1, cols), F32), vmem((n, 1, cols), F32), vmem((ndp, n, 1, cols), F32),
        sem((n,)), sem((n,)), sem((n,)), sem((n,)), sem((n,)), sem((n,)), sem((n,)), sem((n,)),
        sem((rounds, n)), sem((rounds, n)), sem((n,)), sem((n,)), sem((ndp,)), sem((ndp,)), sem((3,)),
    ]
    in_vmem = pl.BlockSpec(memory_space=pltpu.VMEM)
    in_place = pl.BlockSpec(memory_space=pl.ANY)
    unroll = 2
    keys, values, gains = pl.pallas_call(
        functools.partial(kernel, n, ndp, unroll),
        out_shape=(
            jax.ShapeDtypeStruct((n, src, cols), BF16),
            jax.ShapeDtypeStruct((n, src, cols), BF16),
            jax.ShapeDtypeStruct((1, width), F32),
        ),
        in_specs=[in_vmem, in_place, in_vmem, in_vmem, in_vmem],
        out_specs=(in_vmem, in_vmem, in_vmem),
        scratch_shapes=scratch,
        compiler_params=pltpu.CompilerParams(
            collective_id=0, has_side_effects=True, vmem_limit_bytes=60 * 1024 * 1024),
    )(inputs[0, 0], cotangent[0, 0], key_rows[0], value_rows[0], query_gain)
    return keys[None], values[None], gains


def solution(mesh):
    return jax.shard_map(
        on_device,
        mesh=mesh,
        in_specs=(
            P("dp", "section", None, None),
            P("dp", None, None, "section"),
            P("dp", None, None, "section"),
            P("section", None),
            P("dp", "section", None, None),
        ),
        out_specs=(
            P("dp", None, None, "section"),
            P("dp", None, None, "section"),
            P("section", None),
        ),
        check_vma=False,
    )
```

```python
import functools

import jax
import jax.numpy as jnp
from jax import lax
from jax.experimental import pallas as pl
from jax.experimental.pallas import tpu as pltpu
from jax.sharding import PartitionSpec as P

HEAD = 64
TICKS = 3
LANES = 128
MESH = pl.DeviceIdType.MESH
F32 = jnp.float32
BF16 = jnp.bfloat16


def nn(a, b):
    return lax.dot_general(a, b, (((1,), (0,)), ((), ())), preferred_element_type=F32)


def nt(a, b):
    return lax.dot_general(a, b, (((1,), (1,)), ((), ())), preferred_element_type=F32)


def kernel(
    n, ndp, unroll,
    x_ref, ct_ref, k_ref, v_ref, g_ref,
    kout_ref, vout_ref, gout_ref,
    xin, cin, gin, stat, kd, vd, kdt, vdt, gt, xs, qs, probs, plow, raws, ds, grads,
    red, inv, ar, ktot, vtot, gsend, gmid, gdp,
    x_send, x_recv, c_send, c_recv, g_send, g_recv, st_send, st_recv,
    ar_send, ar_recv, gm_send, gm_recv, dp_send, dp_recv, loc,
):
    me = lax.axis_index("section")
    doc = lax.axis_index("dp")
    tok, width = x_ref.shape
    src, cols = k_ref.shape[1], k_ref.shape[2]
    blocks = cols // LANES
    per = LANES // HEAD
    brow = per * src
    scale = HEAD ** (-0.5)

    def peers(body, first=1, last=n):
        def step(j, c):
            body(lax.rem(me + j, n))
            return c
        lax.fori_loop(first, last, step, 0)

    def docs(body):
        def step(j, c):
            body(lax.rem(doc + j, ndp))
            return c
        lax.fori_loop(1, ndp, step, 0)

    def each(body, first=0, last=n, u=None):
        def step(m, c):
            body(m)
            return c
        lax.fori_loop(first, last, step, 0, unroll=u or min(unroll, last - first))

    half = n // 2
    halves = ((0, half), (half, n))

    def to(p, source, target, send, recv):
        return pltpu.make_async_remote_copy(
            src_ref=source, dst_ref=target, send_sem=send, recv_sem=recv,
            device_id={"section": p}, device_id_type=MESH)

    def to_doc(p, source, target, send, recv):
        return pltpu.make_async_remote_copy(
            src_ref=source, dst_ref=target, send_sem=send, recv_sem=recv,
            device_id={"dp": p}, device_id_type=MESH)

    def cut(ref, p):
        return ref.at[:, pl.ds(pl.multiple_of(p * cols, LANES), cols)]

    def x_copy(p, slot):
        return to(p, cut(x_ref, p), xin.at[slot], x_send.at[p], x_recv.at[slot])

    def c_copy(p, slot):
        return to(p, cut(ct_ref, p), cin.at[slot], c_send.at[p], c_recv.at[slot])

    def g_copy(p, slot):
        return to(p, cut(g_ref, p), gin.at[slot], g_send.at[p], g_recv.at[slot])

    def st_copy(p, slot):
        return to(p, stat.at[me], stat.at[slot], st_send.at[p], st_recv.at[slot])

    def ar_copy(a, h, p, slot):
        lo, hi = halves[h]
        return to(p, ar.at[a, me, lo:hi], ar.at[a, slot, lo:hi], ar_send.at[a, h, p], ar_recv.at[a, h, slot])

    def share(a, h):
        peers(lambda p: ar_copy(a, h, p, me).start())

    def gm_copy(p, slot):
        return to(p, gsend.at[p], gmid.at[slot], gm_send.at[p], gm_recv.at[slot])

    def dp_copy(p, slot):
        return to_doc(p, gmid, gdp.at[slot], dp_send.at[p], dp_recv.at[slot])

    barrier = pltpu.get_barrier_semaphore()
    peers(lambda p: pl.semaphore_signal(barrier, inc=1, device_id={"section": p}, device_id_type=MESH))
    docs(lambda p: pl.semaphore_signal(barrier, inc=1, device_id={"dp": p}, device_id_type=MESH))

    total = jnp.zeros((tok, LANES), F32)
    for b in range(width // LANES):
        part = x_ref[:, b * LANES:(b + 1) * LANES].astype(F32)
        total = total + part * part
    stat[me] = jnp.sum(total.T, axis=0, keepdims=True)

    pl.semaphore_wait(barrier, n + ndp - 2)

    peers(lambda p: g_copy(p, me).start())
    peers(lambda p: st_copy(p, me).start())
    peers(lambda p: x_copy(p, me).start())
    first_cut, second_cut = (1 + n) // 4, 1 + (5 * n) // 8
    peers(lambda p: c_copy(p, me).start(), 1, first_cut)
    own = [
        pltpu.make_async_copy(cut(g_ref, me), gin.at[me], loc.at[0]),
        pltpu.make_async_copy(cut(x_ref, me), xin.at[me], loc.at[1]),
        pltpu.make_async_copy(cut(ct_ref, me), cin.at[me], loc.at[2]),
    ]
    for copy in own:
        copy.start()

    lane = lax.broadcasted_iota(jnp.int32, (src, LANES), 1)
    sides = [jnp.logical_and(lane >= i * HEAD, lane < (i + 1) * HEAD) for i in range(per)]

    def spread(l):
        for source, plain, turned in ((k_ref, kd, kdt), (v_ref, vd, vdt)):
            rows = source[l].astype(F32)
            for b in range(blocks):
                piece = rows[:, b * LANES:(b + 1) * LANES]
                both = jnp.concatenate([jnp.where(s, piece, 0.0) for s in sides], axis=0)
                plain[l, b] = both.astype(BF16)
                turned[l, b] = both.T.astype(BF16)
        ktot[l] = jnp.zeros((src, cols), F32)
        vtot[l] = jnp.zeros((src, cols), F32)

    each(spread, u=2)

    own[0].wait()
    peers(lambda p: g_copy(p, p).wait_recv())

    def turn_gain(l):
        for b in range(blocks):
            row = gin[l, :, b * LANES:(b + 1) * LANES]
            gt[l, b * LANES:(b + 1) * LANES, :] = jnp.broadcast_to(row, (LANES, LANES)).T

    each(turn_gain, u=2)
    peers(lambda p: st_copy(p, p).wait_recv())

    def fwd(k, m, more):
        l = lax.rem(m + k, n)
        factor = inv[k, m]
        pieces = []
        sums = jnp.zeros((1, tok), F32)
        for b in range(blocks):
            at = slice(b * LANES, (b + 1) * LANES)
            rows = slice(b * brow, (b + 1) * brow)
            xf = xs[k, m, at, :].astype(F32)
            q = (xf * factor * gt[l, at, :]).astype(BF16)
            qs[k, m, at, :] = q
            raw = nn(kd[l, b], q)
            raws[k, m, rows, :] = raw
            s3 = raw.reshape(per, src, tok) * scale
            w = jnp.exp(s3 - jnp.max(s3, axis=1, keepdims=True))
            p = w * (1.0 / jnp.sum(w, axis=1, keepdims=True))
            p = p.reshape(brow, tok)
            probs[k, m, rows, :] = p
            low = p.astype(BF16)
            plow[k, m, rows, :] = low
            if more:
                y = (xf + nn(vdt[l, b], low)).astype(BF16)
                xs[k + 1, m, at, :] = y
                yf = y.astype(F32)
                sums = sums + jnp.sum(yf * yf, axis=0, keepdims=True)
        if more:
            ar[k, me, m] = sums

    def reduced(a, h):
        lo, hi = halves[h]
        peers(lambda p: ar_copy(a, h, p, p).wait_recv())
        total = ar[a, 0, lo:hi]
        for s in range(1, n):
            total = total + ar[a, s, lo:hi]
        return total * (1.0 / width)

    def arrive(j, c):
        m = lax.rem(me + j, n)

        @pl.when(j == 0)
        def _():
            own[1].wait()

        @pl.when(j > 0)
        def _():
            x_copy(m, m).wait_recv()

        inv[0, m] = lax.rsqrt(stat[m] * (1.0 / width) + 1e-6)
        for b in range(blocks):
            at = slice(b * LANES, (b + 1) * LANES)
            xs[0, m, at, :] = xin[m, :, at].T
        fwd(0, m, True)
        return c

    lax.fori_loop(0, n, arrive, 0)
    share(0, 0)
    share(0, 1)
    peers(lambda p: c_copy(p, me).start(), first_cut, second_cut)
    for k in range(1, TICKS):
        for h, (lo, hi) in enumerate(halves):
            inv[k, lo:hi] = lax.rsqrt(reduced(k - 1, h) + 1e-6)
            each(lambda m: fwd(k, m, k + 1 < TICKS), lo, hi)
            if k + 1 < TICKS:
                share(k, h)
        if k == 1:
            peers(lambda p: c_copy(p, me).start(), second_cut, n)

    own[2].wait()

    def arrive_c(p):
        c_copy(p, p).wait_recv()

    def turn_c(m):
        s = lax.rem(m + TICKS, n)
        for b in range(blocks):
            at = slice(b * LANES, (b + 1) * LANES)
            grads[TICKS - 1, m, at, :] = cin[s, :, at].T

    peers(arrive_c)

    def scores_back(k, a, m):
        l = lax.rem(m + k, n)
        sums = jnp.zeros((1, tok), F32)
        for b in range(blocks):
            at = slice(b * LANES, (b + 1) * LANES)
            rows = slice(b * brow, (b + 1) * brow)
            dprob = nn(vd[l, b], grads[k, m, at, :]).reshape(per, src, tok)
            p = probs[k, m, rows, :].reshape(per, src, tok)
            mean = jnp.sum(p * dprob, axis=1, keepdims=True)
            d = (p * (dprob - mean) * scale).reshape(brow, tok).astype(BF16)
            ds[k, m, rows, :] = d
            if a is not None:
                sums = sums + jnp.sum(d.astype(F32) * raws[k, m, rows, :], axis=0, keepdims=True)
        if a is not None:
            ar[a, me, m] = sums

    def picked(r):
        out = r[:src]
        for i in range(1, per):
            out = jnp.where(sides[i], r[i * src:(i + 1) * src], out)
        return out

    def key_step(k, m):
        l = lax.rem(m + k, n)
        for b in range(blocks):
            at = slice(b * LANES, (b + 1) * LANES)
            rows = slice(b * brow, (b + 1) * brow)
            ktot[l, :, at] += picked(nt(ds[k, m, rows, :], qs[k, m, at, :]))

    def value_step(k, m):
        l = lax.rem(m + k, n)
        for b in range(blocks):
            at = slice(b * LANES, (b + 1) * LANES)
            rows = slice(b * brow, (b + 1) * brow)
            vtot[l, :, at] += picked(nt(plow[k, m, rows, :], grads[k, m, at, :]))

    def input_back(k, m):
        l = lax.rem(m + k, n)
        factor = inv[k, m]
        mean = red[m]
        for b in range(blocks):
            at = slice(b * LANES, (b + 1) * LANES)
            rows = slice(b * brow, (b + 1) * brow)
            dq = nn(kdt[l, b], ds[k, m, rows, :])
            u = xs[k, m, at, :].astype(F32) * factor
            back = grads[k, m, at, :].astype(F32) + factor * (gt[l, at, :] * dq - u * mean)
            grads[k - 1, m, at, :] = back.astype(BF16)

    def start_back(m):
        turn_c(m)
        scores_back(TICKS - 1, 2 * TICKS - 3, m)

    for h, (lo, hi) in enumerate(halves):
        each(start_back, lo, hi)
        share(2 * TICKS - 3, h)
    for k in range(TICKS - 1, 0, -1):
        a = TICKS - 1 + k - 1

        def next_back(m):
            input_back(k, m)
            scores_back(k - 1, a - 1 if k > 1 else None, m)

        each(lambda m: key_step(k, m))
        for h, (lo, hi) in enumerate(halves):
            red[lo:hi] = reduced(a, h)
            each(next_back, lo, hi)
            if k > 1:
                share(a - 1, h)

    def last(m):
        key_step(0, m)
        steps = ktot[m]
        kout_ref[m] = steps.astype(BF16)
        gsend[m] = jnp.sum(steps * k_ref[m].astype(F32), axis=0, keepdims=True) / gin[m]

    each(last)
    peers(lambda p: gm_copy(p, me).start())
    gmid[me] = gsend[me]

    each(lambda m: value_step(TICKS - 1, m))
    for k in range(1, TICKS - 1):
        each(lambda m: value_step(k, m))
    peers(lambda p: gm_copy(p, p).wait_recv())
    docs(lambda p: dp_copy(p, doc).start())

    def finish(m):
        value_step(0, m)
        vout_ref[m] = vtot[m].astype(BF16)

    each(finish)

    def drain(p):
        x_copy(p, me).wait_send()
        c_copy(p, me).wait_send()
        g_copy(p, me).wait_send()
        st_copy(p, me).wait_send()
        for a in range(2 * (TICKS - 1)):
            for h in range(2):
                ar_copy(a, h, p, me).wait_send()
        gm_copy(p, me).wait_send()

    peers(drain)
    gdp[doc] = gmid[...]
    docs(lambda p: dp_copy(p, p).wait_recv())
    docs(lambda p: dp_copy(p, doc).wait_send())
    for s in range(n):
        out = gdp[0, s]
        for d in range(1, ndp):
            out = out + gdp[d, s]
        gout_ref[:, s * cols:(s + 1) * cols] = out


def on_device(inputs, key_rows, value_rows, query_gain, cotangent):
    n = lax.axis_size("section")
    ndp = lax.axis_size("dp")
    tok, width = inputs.shape[2:]
    src, cols = key_rows.shape[2:]
    blocks = cols // LANES
    brow = LANES // HEAD * src
    rows = blocks * brow
    rounds = 2 * (TICKS - 1)
    vmem = pltpu.VMEM
    sem = pltpu.SemaphoreType.DMA
    scratch = [
        vmem((n, tok, cols), BF16), vmem((n, tok, cols), BF16),
        vmem((n, 1, cols), F32), vmem((n, 1, tok), F32),
        vmem((n, blocks, brow, LANES), BF16), vmem((n, blocks, brow, LANES), BF16),
        vmem((n, blocks, LANES, brow), BF16), vmem((n, blocks, LANES, brow), BF16),
        vmem((n, cols, LANES), F32),
        vmem((TICKS, n, cols, tok), BF16), vmem((TICKS, n, cols, tok), BF16),
        vmem((TICKS, n, rows, tok), F32), vmem((TICKS, n, rows, tok), BF16),
        vmem((TICKS, n, rows, tok), F32),
        vmem((TICKS, n, rows, tok), BF16), vmem((TICKS, n, cols, tok), BF16),
        vmem((n, 1, tok), F32), vmem((TICKS, n, 1, tok), F32),
        vmem((rounds, n, n, 1, tok), F32),
        vmem((n, src, cols), F32), vmem((n, src, cols), F32),
        vmem((n, 1, cols), F32), vmem((n, 1, cols), F32), vmem((ndp, n, 1, cols), F32),
        sem((n,)), sem((n,)), sem((n,)), sem((n,)), sem((n,)), sem((n,)), sem((n,)), sem((n,)),
        sem((rounds, 2, n)), sem((rounds, 2, n)), sem((n,)), sem((n,)), sem((ndp,)), sem((ndp,)), sem((3,)),
    ]
    in_vmem = pl.BlockSpec(memory_space=pltpu.VMEM)
    in_place = pl.BlockSpec(memory_space=pl.ANY)
    unroll = 8
    keys, values, gains = pl.pallas_call(
        functools.partial(kernel, n, ndp, unroll),
        out_shape=(
            jax.ShapeDtypeStruct((n, src, cols), BF16),
            jax.ShapeDtypeStruct((n, src, cols), BF16),
            jax.ShapeDtypeStruct((1, width), F32),
        ),
        in_specs=[in_vmem, in_place, in_vmem, in_vmem, in_vmem],
        out_specs=(in_vmem, in_vmem, in_vmem),
        scratch_shapes=scratch,
        compiler_params=pltpu.CompilerParams(
            collective_id=0, has_side_effects=True, vmem_limit_bytes=60 * 1024 * 1024),
    )(inputs[0, 0], cotangent[0, 0], key_rows[0], value_rows[0], query_gain)
    return keys[None], values[None], gains


def solution(mesh):
    return jax.shard_map(
        on_device,
        mesh=mesh,
        in_specs=(
            P("dp", "section", None, None),
            P("dp", None, None, "section"),
            P("dp", None, None, "section"),
            P("section", None),
            P("dp", "section", None, None),
        ),
        out_specs=(
            P("dp", None, None, "section"),
            P("dp", None, None, "section"),
            P("section", None),
        ),
        check_vma=False,
    )
```

```python
import functools

import jax
import jax.numpy as jnp
from jax import lax
from jax.experimental import pallas as pl
from jax.experimental.pallas import tpu as pltpu
from jax.sharding import PartitionSpec as P

HEAD = 64
TICKS = 3
LANES = 128
MESH = pl.DeviceIdType.MESH
F32 = jnp.float32
BF16 = jnp.bfloat16


def nn(a, b):
    return lax.dot_general(a, b, (((1,), (0,)), ((), ())), preferred_element_type=F32)


def nt(a, b):
    return lax.dot_general(a, b, (((1,), (1,)), ((), ())), preferred_element_type=F32)


def kernel(
    n, ndp, unroll,
    x_ref, ct_ref, k_ref, v_ref, g_ref,
    kout_ref, vout_ref, gout_ref,
    xin, cin, gin, stat, kd, vd, kdt, vdt, gt, xs, qs, probs, plow, raws, ds, grads,
    red, inv, ar, ktot, vtot, gsend, gdp,
    x_send, x_recv, c_send, c_recv, g_send, g_recv, st_send, st_recv,
    ar_send, ar_recv, dp_send, dp_recv, loc,
):
    me = lax.axis_index("section")
    doc = lax.axis_index("dp")
    tok, width = x_ref.shape
    src, cols = k_ref.shape[1], k_ref.shape[2]
    blocks = cols // LANES
    per = LANES // HEAD
    brow = per * src
    scale = HEAD ** (-0.5)

    def peers(body, first=1, last=n):
        def step(j, c):
            body(lax.rem(me + j, n))
            return c
        lax.fori_loop(first, last, step, 0)

    def each(body, first=0, last=n, u=None):
        def step(m, c):
            body(m)
            return c
        lax.fori_loop(first, last, step, 0, unroll=u or min(unroll, last - first))

    half = n // 2
    halves = ((0, half), (half, n))

    def to(p, source, target, send, recv):
        return pltpu.make_async_remote_copy(
            src_ref=source, dst_ref=target, send_sem=send, recv_sem=recv,
            device_id={"section": p}, device_id_type=MESH)

    def others(body):
        def step(j, c):
            place = lax.rem(doc * n + me + j, n * ndp)
            body(lax.div(place, n), lax.rem(place, n))
            return c
        lax.fori_loop(1, n * ndp, step, 0)

    def cut(ref, p):
        return ref.at[:, pl.ds(pl.multiple_of(p * cols, LANES), cols)]

    def x_copy(p, slot):
        return to(p, cut(x_ref, p), xin.at[slot], x_send.at[p], x_recv.at[slot])

    def c_copy(p, slot):
        return to(p, cut(ct_ref, p), cin.at[slot], c_send.at[p], c_recv.at[slot])

    def g_copy(p, slot):
        return to(p, cut(g_ref, p), gin.at[slot], g_send.at[p], g_recv.at[slot])

    def st_copy(p, slot):
        return to(p, stat.at[me], stat.at[slot], st_send.at[p], st_recv.at[slot])

    def ar_copy(a, h, p, slot):
        lo, hi = halves[h]
        return to(p, ar.at[a, me, lo:hi], ar.at[a, slot, lo:hi], ar_send.at[a, h, p], ar_recv.at[a, h, slot])

    def share(a, h):
        peers(lambda p: ar_copy(a, h, p, me).start())

    def dp_copy(q, p, from_doc, slot):
        return pltpu.make_async_remote_copy(
            src_ref=gsend.at[p], dst_ref=gdp.at[from_doc, slot],
            send_sem=dp_send.at[q, p], recv_sem=dp_recv.at[from_doc, slot],
            device_id={"dp": q, "section": p}, device_id_type=MESH)

    barrier = pltpu.get_barrier_semaphore()
    others(lambda q, p: pl.semaphore_signal(
        barrier, inc=1, device_id={"dp": q, "section": p}, device_id_type=MESH))

    total = jnp.zeros((tok, LANES), F32)
    for b in range(width // LANES):
        part = x_ref[:, b * LANES:(b + 1) * LANES].astype(F32)
        total = total + part * part
    stat[me] = jnp.sum(total.T, axis=0, keepdims=True)

    pl.semaphore_wait(barrier, n * ndp - 1)

    peers(lambda p: g_copy(p, me).start())
    peers(lambda p: st_copy(p, me).start())
    peers(lambda p: x_copy(p, me).start())
    first_cut, second_cut = (1 + n) // 4, 1 + (5 * n) // 8
    peers(lambda p: c_copy(p, me).start(), 1, first_cut)
    own = [
        pltpu.make_async_copy(cut(g_ref, me), gin.at[me], loc.at[0]),
        pltpu.make_async_copy(cut(x_ref, me), xin.at[me], loc.at[1]),
        pltpu.make_async_copy(cut(ct_ref, me), cin.at[me], loc.at[2]),
    ]
    for copy in own:
        copy.start()

    lane = lax.broadcasted_iota(jnp.int32, (src, LANES), 1)
    sides = [jnp.logical_and(lane >= i * HEAD, lane < (i + 1) * HEAD) for i in range(per)]

    def spread(l):
        for source, plain, turned in ((k_ref, kd, kdt), (v_ref, vd, vdt)):
            rows = source[l].astype(F32)
            for b in range(blocks):
                piece = rows[:, b * LANES:(b + 1) * LANES]
                both = jnp.concatenate([jnp.where(s, piece, 0.0) for s in sides], axis=0)
                plain[l, b] = both.astype(BF16)
                turned[l, b] = both.T.astype(BF16)
        ktot[l] = jnp.zeros((src, cols), F32)
        vtot[l] = jnp.zeros((src, cols), F32)

    each(spread, u=2)

    own[0].wait()
    peers(lambda p: g_copy(p, p).wait_recv())

    def turn_gain(l):
        for b in range(blocks):
            row = gin[l, :, b * LANES:(b + 1) * LANES]
            gt[l, b * LANES:(b + 1) * LANES, :] = jnp.broadcast_to(row, (LANES, LANES)).T

    each(turn_gain, u=2)
    peers(lambda p: st_copy(p, p).wait_recv())

    def fwd(k, m, more):
        l = lax.rem(m + k, n)
        factor = inv[k, m]
        pieces = []
        sums = jnp.zeros((1, tok), F32)
        for b in range(blocks):
            at = slice(b * LANES, (b + 1) * LANES)
            rows = slice(b * brow, (b + 1) * brow)
            xf = xs[k, m, at, :].astype(F32)
            q = (xf * factor * gt[l, at, :]).astype(BF16)
            qs[k, m, at, :] = q
            raw = nn(kd[l, b], q)
            raws[k, m, rows, :] = raw
            s3 = raw.reshape(per, src, tok) * scale
            w = jnp.exp(s3 - jnp.max(s3, axis=1, keepdims=True))
            p = w * (1.0 / jnp.sum(w, axis=1, keepdims=True))
            p = p.reshape(brow, tok)
            probs[k, m, rows, :] = p
            low = p.astype(BF16)
            plow[k, m, rows, :] = low
            if more:
                y = (xf + nn(vdt[l, b], low)).astype(BF16)
                xs[k + 1, m, at, :] = y
                yf = y.astype(F32)
                sums = sums + jnp.sum(yf * yf, axis=0, keepdims=True)
        if more:
            ar[k, me, m] = sums

    def reduced(a, h):
        lo, hi = halves[h]
        peers(lambda p: ar_copy(a, h, p, p).wait_recv())
        total = ar[a, 0, lo:hi]
        for s in range(1, n):
            total = total + ar[a, s, lo:hi]
        return total * (1.0 / width)

    def arrive(j, c):
        m = lax.rem(me + j, n)

        @pl.when(j == 0)
        def _():
            own[1].wait()

        @pl.when(j > 0)
        def _():
            x_copy(m, m).wait_recv()

        inv[0, m] = lax.rsqrt(stat[m] * (1.0 / width) + 1e-6)
        for b in range(blocks):
            at = slice(b * LANES, (b + 1) * LANES)
            xs[0, m, at, :] = xin[m, :, at].T
        fwd(0, m, True)
        return c

    lax.fori_loop(0, n, arrive, 0)
    share(0, 0)
    share(0, 1)
    peers(lambda p: c_copy(p, me).start(), first_cut, second_cut)
    for k in range(1, TICKS):
        for h, (lo, hi) in enumerate(halves):
            inv[k, lo:hi] = lax.rsqrt(reduced(k - 1, h) + 1e-6)
            each(lambda m: fwd(k, m, k + 1 < TICKS), lo, hi)
            if k + 1 < TICKS:
                share(k, h)
        if k == 1:
            peers(lambda p: c_copy(p, me).start(), second_cut, n)

    own[2].wait()

    def arrive_c(p):
        c_copy(p, p).wait_recv()

    def turn_c(m):
        s = lax.rem(m + TICKS, n)
        for b in range(blocks):
            at = slice(b * LANES, (b + 1) * LANES)
            grads[TICKS - 1, m, at, :] = cin[s, :, at].T

    peers(arrive_c)

    def scores_back(k, a, m):
        l = lax.rem(m + k, n)
        sums = jnp.zeros((1, tok), F32)
        for b in range(blocks):
            at = slice(b * LANES, (b + 1) * LANES)
            rows = slice(b * brow, (b + 1) * brow)
            dprob = nn(vd[l, b], grads[k, m, at, :]).reshape(per, src, tok)
            p = probs[k, m, rows, :].reshape(per, src, tok)
            mean = jnp.sum(p * dprob, axis=1, keepdims=True)
            d = (p * (dprob - mean) * scale).reshape(brow, tok).astype(BF16)
            ds[k, m, rows, :] = d
            if a is not None:
                sums = sums + jnp.sum(d.astype(F32) * raws[k, m, rows, :], axis=0, keepdims=True)
        if a is not None:
            ar[a, me, m] = sums

    def picked(r):
        out = r[:src]
        for i in range(1, per):
            out = jnp.where(sides[i], r[i * src:(i + 1) * src], out)
        return out

    def key_step(k, m):
        l = lax.rem(m + k, n)
        for b in range(blocks):
            at = slice(b * LANES, (b + 1) * LANES)
            rows = slice(b * brow, (b + 1) * brow)
            ktot[l, :, at] += picked(nt(ds[k, m, rows, :], qs[k, m, at, :]))

    def value_step(k, m):
        l = lax.rem(m + k, n)
        for b in range(blocks):
            at = slice(b * LANES, (b + 1) * LANES)
            rows = slice(b * brow, (b + 1) * brow)
            vtot[l, :, at] += picked(nt(plow[k, m, rows, :], grads[k, m, at, :]))

    def input_back(k, m):
        l = lax.rem(m + k, n)
        factor = inv[k, m]
        mean = red[m]
        for b in range(blocks):
            at = slice(b * LANES, (b + 1) * LANES)
            rows = slice(b * brow, (b + 1) * brow)
            dq = nn(kdt[l, b], ds[k, m, rows, :])
            u = xs[k, m, at, :].astype(F32) * factor
            back = grads[k, m, at, :].astype(F32) + factor * (gt[l, at, :] * dq - u * mean)
            grads[k - 1, m, at, :] = back.astype(BF16)

    def start_back(m):
        turn_c(m)
        scores_back(TICKS - 1, 2 * TICKS - 3, m)

    for h, (lo, hi) in enumerate(halves):
        each(start_back, lo, hi)
        share(2 * TICKS - 3, h)
    for k in range(TICKS - 1, 0, -1):
        a = TICKS - 1 + k - 1

        def next_back(m):
            input_back(k, m)
            scores_back(k - 1, a - 1 if k > 1 else None, m)

        each(lambda m: key_step(k, m))
        for h, (lo, hi) in enumerate(halves):
            red[lo:hi] = reduced(a, h)
            each(next_back, lo, hi)
            if k > 1:
                share(a - 1, h)

    def last(m):
        key_step(0, m)
        steps = ktot[m]
        kout_ref[m] = steps.astype(BF16)
        gsend[m] = jnp.sum(steps * k_ref[m].astype(F32), axis=0, keepdims=True) / gin[m]

    each(last)
    others(lambda q, p: dp_copy(q, p, doc, me).start())
    gdp[doc, me] = gsend[me]

    each(lambda m: value_step(TICKS - 1, m))
    for k in range(1, TICKS - 1):
        each(lambda m: value_step(k, m))

    def finish(m):
        value_step(0, m)
        vout_ref[m] = vtot[m].astype(BF16)

    each(finish)

    def drain(p):
        x_copy(p, me).wait_send()
        c_copy(p, me).wait_send()
        g_copy(p, me).wait_send()
        st_copy(p, me).wait_send()
        for a in range(2 * (TICKS - 1)):
            for h in range(2):
                ar_copy(a, h, p, me).wait_send()

    peers(drain)
    others(lambda q, p: dp_copy(q, p, q, p).wait_recv())
    others(lambda q, p: dp_copy(q, p, doc, me).wait_send())
    for s in range(n):
        out = gdp[0, s]
        for d in range(1, ndp):
            out = out + gdp[d, s]
        gout_ref[:, s * cols:(s + 1) * cols] = out


def on_device(inputs, key_rows, value_rows, query_gain, cotangent):
    n = lax.axis_size("section")
    ndp = lax.axis_size("dp")
    tok, width = inputs.shape[2:]
    src, cols = key_rows.shape[2:]
    blocks = cols // LANES
    brow = LANES // HEAD * src
    rows = blocks * brow
    rounds = 2 * (TICKS - 1)
    vmem = pltpu.VMEM
    sem = pltpu.SemaphoreType.DMA
    scratch = [
        vmem((n, tok, cols), BF16), vmem((n, tok, cols), BF16),
        vmem((n, 1, cols), F32), vmem((n, 1, tok), F32),
        vmem((n, blocks, brow, LANES), BF16), vmem((n, blocks, brow, LANES), BF16),
        vmem((n, blocks, LANES, brow), BF16), vmem((n, blocks, LANES, brow), BF16),
        vmem((n, cols, LANES), F32),
        vmem((TICKS, n, cols, tok), BF16), vmem((TICKS, n, cols, tok), BF16),
        vmem((TICKS, n, rows, tok), F32), vmem((TICKS, n, rows, tok), BF16),
        vmem((TICKS, n, rows, tok), F32),
        vmem((TICKS, n, rows, tok), BF16), vmem((TICKS, n, cols, tok), BF16),
        vmem((n, 1, tok), F32), vmem((TICKS, n, 1, tok), F32),
        vmem((rounds, n, n, 1, tok), F32),
        vmem((n, src, cols), F32), vmem((n, src, cols), F32),
        vmem((n, 1, cols), F32), vmem((ndp, n, 1, cols), F32),
        sem((n,)), sem((n,)), sem((n,)), sem((n,)), sem((n,)), sem((n,)), sem((n,)), sem((n,)),
        sem((rounds, 2, n)), sem((rounds, 2, n)), sem((ndp, n)), sem((ndp, n)), sem((3,)),
    ]
    in_vmem = pl.BlockSpec(memory_space=pltpu.VMEM)
    in_place = pl.BlockSpec(memory_space=pl.ANY)
    unroll = 8
    keys, values, gains = pl.pallas_call(
        functools.partial(kernel, n, ndp, unroll),
        out_shape=(
            jax.ShapeDtypeStruct((n, src, cols), BF16),
            jax.ShapeDtypeStruct((n, src, cols), BF16),
            jax.ShapeDtypeStruct((1, width), F32),
        ),
        in_specs=[in_vmem, in_place, in_vmem, in_vmem, in_vmem],
        out_specs=(in_vmem, in_vmem, in_vmem),
        scratch_shapes=scratch,
        compiler_params=pltpu.CompilerParams(
            collective_id=0, has_side_effects=True, vmem_limit_bytes=60 * 1024 * 1024),
    )(inputs[0, 0], cotangent[0, 0], key_rows[0], value_rows[0], query_gain)
    return keys[None], values[None], gains


def solution(mesh):
    return jax.shard_map(
        on_device,
        mesh=mesh,
        in_specs=(
            P("dp", "section", None, None),
            P("dp", None, None, "section"),
            P("dp", None, None, "section"),
            P("section", None),
            P("dp", "section", None, None),
        ),
        out_specs=(
            P("dp", None, None, "section"),
            P("dp", None, None, "section"),
            P("section", None),
        ),
        check_vma=False,
    )
```
